32 devices in a mesh: line: 2 (over y), bin: 16 (over z, x, core).
Axes of the slice: x: 2, y: 2, z: 4, core: 2. Of those that a mesh axis runs over, the one named last changes fastest.
Arguments:
- predicted: bfloat16 [4096, 2048], P(('line', 'bin')), parts along dimension 0, may hold values from -1200 to 1200
- observed: float32 [4096, 2048], P(('line', 'bin')), parts along dimension 0, may hold values from -1200 to 1200
- data_weight: float32 [4096, 2048], P(('line', 'bin')), parts along dimension 0, may hold values from 0.5 to 2
- bin_ids: int32 [4096], P(('line', 'bin')), parts along dimension 0, may hold values from 0 to 31, as said below
- offset_slots: int32 [4096], P(('line', 'bin')), parts along dimension 0, may hold values from 0 to 63, as said below
- conv_in: bfloat16 [3, 3, 48], replicated, may hold values from -2 to 2
- conv_mid: bfloat16 [3, 3, 48, 48], replicated, may hold values from -0.3125 to 0.3125
- conv_out: bfloat16 [3, 3, 48], replicated, may hold values from -0.3125 to 0.3125
Outputs:
- residual_traces: bfloat16 [4096, 2048], P(('line', 'bin')), parts along dimension 0
The draws below stay inside these ranges and needn't reach their ends.
There are 2 independent parts, one for each index of `line`. The reference program is written for one: setup_inputs(seed, part) draws one part's arguments, and reference() takes and returns one part's arrays. A program takes and returns all parts, laid end to end along the dimension named above; an argument that names none is the same for every part. Nothing has to cross between parts.
Inputs may be any that keep to these rules, and one draw needn't show every extreme that they name: `bin_ids`: bin b belongs to index b // 2 of bin. The traces of one device go at most 16 to one owner and at most 8 to one bin, both reached in every draw. Taken by owner index minus the sender's index, modulo the devices of bin, every device sends the same counts. Every owner receives exactly 128 traces, 64 in each of its bins. `offset_slots`: no two traces have the same bin and slot.
All inputs are finite; a program needn't handle non-finite values.
Results may differ from the reference program's by a relative error of at most 0.0065.
Values may be sent and summed in bfloat16 or wider, within the bound.
A program may use at most 256 MiB of HBM per device.

```python
import math
import jax
import jax.numpy as jnp
from jax import lax

NT = 2048
CHAN = 48
OFFS = 64
TR_DEV = 128
TRACES = 2048
BIN_DEV = 2
BINS = 32
CAP = 16


def trace_layout(key):
    owners = TRACES // TR_DEV
    light = max(1, TR_DEV // owners)
    heavy = TR_DEV // (2 * CAP)
    spread = TR_DEV // 2 // light
    base = jax.random.fold_in(key, 11)
    key_order, key_bins, key_slots, key_rows = jax.random.split(base, 4)
    order = jax.random.permutation(key_order, owners).astype(jnp.int32)
    counts = jnp.where(order < heavy, CAP, jnp.where(order < heavy + spread, light, 0)).astype(jnp.int32)
    bounds = jnp.cumsum(counts)
    row_index = jnp.arange(TR_DEV, dtype=jnp.int32)
    distance = jnp.sum((bounds[None, :] <= row_index[:, None]).astype(jnp.int32), axis=1)
    sender = jnp.arange(owners, dtype=jnp.int32)[:, None]
    owner_dev = (sender + distance[None, :]) % owners
    raw_bin = row_index % BIN_DEV
    raw_slot = row_index // BIN_DEV
    bin_perm = jax.vmap(lambda sub_key: jax.random.permutation(sub_key, BIN_DEV))(jax.random.split(key_bins, owners)).astype(jnp.int32)
    scores = jax.random.randint(key_slots, (owners, BIN_DEV, OFFS), 2, 1 << 20) * OFFS + jnp.arange(OFFS, dtype=jnp.int32)
    scores = scores.at[:, :, OFFS - 1].set(0).at[:, :, 0].set(1)
    slot_perm = jnp.argsort(scores, axis=-1).astype(jnp.int32)
    local_bin = bin_perm[owner_dev, raw_bin[None, :]]
    slot_value = slot_perm[owner_dev, raw_bin[None, :], raw_slot[None, :]]
    bin_value = owner_dev * BIN_DEV + local_bin
    row_perm = jax.vmap(lambda sub_key: jax.random.permutation(sub_key, TR_DEV))(jax.random.split(key_rows, owners)).astype(jnp.int32)
    bin_value = jnp.take_along_axis(bin_value, row_perm, axis=1)
    slot_value = jnp.take_along_axis(slot_value, row_perm, axis=1)
    return (bin_value.reshape(-1).astype(jnp.int32), slot_value.reshape(-1).astype(jnp.int32))


def draw_bin_ids(key, part):
    return trace_layout(key)[0]


def draw_offset_slots(key, part):
    return trace_layout(key)[1]


def trace_scales(key):
    key_rows, key_cols = jax.random.split(jax.random.fold_in(key, 21))
    position = jnp.arange(TRACES, dtype=jnp.float32) / TRACES
    top = 10.0
    row_scale = jnp.exp(jax.random.uniform(key_rows, (TRACES,)) * math.log(top)) * (1.0 + 0.75 * position)
    col_scale = jnp.exp(jax.random.uniform(key_cols, (NT,)) * math.log(10.0))
    return (row_scale, col_scale)


def rough_field(key):
    field = jax.random.normal(key, (TRACES, NT))
    return jnp.clip(field, -4.0, 4.0)


def draw_predicted(key, part):
    row_scale, col_scale = trace_scales(key)
    field = rough_field(jax.random.fold_in(key, 31))
    return (field * row_scale[:, None] * col_scale[None, :]).astype(jnp.bfloat16)


def draw_observed(key, part):
    row_scale, col_scale = trace_scales(key)
    field = rough_field(jax.random.fold_in(key, 41))
    return (field * row_scale[:, None] * col_scale[None, :]).astype(jnp.float32)


def block_scale(own_key, extent, shards, smallest, high):
    factor_of, own = 1.0, jax.random.fold_in(own_key, 6)
    for dim, shards_of in shards:
        steps = jnp.exp(jax.random.uniform(jax.random.fold_in(own, dim), (shards_of,), jnp.float32, smallest / len(shards), high / len(shards)))
        factor_of = factor_of * jnp.repeat(steps, extent[dim] // shards_of).reshape([-1 if axis == dim else 1 for axis in range(len(extent))])
    return factor_of


def centred(key, extent, scale, bound, held_as=jnp.bfloat16):
    result = scale * jax.random.normal(key, extent, jnp.float32)
    return jnp.clip(result, min=-bound, max=bound).astype(held_as)


def setup_inputs(seed: int = 0, part: int = 0) -> dict:
    seeds = jax.random.split(jax.random.key(seed), 9)
    own_keys = jax.random.split(jax.random.fold_in(seeds[8], part), 9)
    predicted = draw_predicted(jax.random.fold_in(jax.random.fold_in(seeds[8], part), 71), part)
    observed = draw_observed(jax.random.fold_in(jax.random.fold_in(seeds[8], part), 71), part)
    data_weight = jnp.clip(jnp.exp(math.log(2.0) - 1.3862944 * jax.random.uniform(own_keys[2], (TRACES, NT), jnp.float32) ** block_scale(own_keys[2], (TRACES, NT), ((0, 16),), -0.2, 0.2)), 0.5, 2.0)
    bin_ids = draw_bin_ids(jax.random.fold_in(jax.random.fold_in(seeds[8], part), 71), part)
    offset_slots = draw_offset_slots(jax.random.fold_in(jax.random.fold_in(seeds[8], part), 71), part)
    conv_in = centred(seeds[5], (3, 3, CHAN), 9 ** -0.5, 2.0)
    conv_mid = centred(seeds[6], (3, 3, CHAN, CHAN), (9 * CHAN) ** -0.5, 0.3125)
    conv_out = centred(seeds[7], (3, 3, CHAN), (9 * CHAN) ** -0.5, 0.3125)
    return {"predicted": predicted, "observed": observed, "data_weight": data_weight, "bin_ids": bin_ids, "offset_slots": offset_slots, "conv_in": conv_in, "conv_mid": conv_mid, "conv_out": conv_out}


def shifted(values, along_offset, along_time):
    last = values.ndim - 1
    span_x = values.shape[-2]
    span_t = values.shape[-1]
    pad_x = abs(along_offset)
    pad_t = abs(along_time)
    widths = [(0, 0)] * (values.ndim - 2) + [(pad_x, pad_x), (pad_t, pad_t)]
    padded = jnp.pad(values, widths)
    padded = lax.slice_in_dim(padded, pad_x + along_offset, pad_x + along_offset + span_x, axis=last - 1)
    return lax.slice_in_dim(padded, pad_t + along_time, pad_t + along_time + span_t, axis=last)

def network(panel, conv_in, conv_mid, conv_out):
    values = panel.astype(jnp.float32)
    first_sum = jnp.zeros((CHAN,) + values.shape, jnp.float32)
    for row_tap in range(3):
        for time_tap in range(3):
            weights = conv_in[row_tap, time_tap].astype(jnp.float32)
            first_sum = first_sum + weights[:, None, None] * shifted(values, row_tap - 1, time_tap - 1)[None]
    first_hidden = jax.nn.silu(first_sum).astype(jnp.bfloat16)
    first_wide = first_hidden.astype(jnp.float32)
    second_sum = jnp.zeros((CHAN,) + values.shape, jnp.float32)
    for row_tap in range(3):
        for time_tap in range(3):
            second_sum = second_sum + jnp.einsum('io,ixt->oxt', conv_mid[row_tap, time_tap].astype(jnp.float32), shifted(first_wide, 2 * (row_tap - 1), 4 * (time_tap - 1)), precision=lax.Precision.HIGHEST)
    second_hidden = (first_wide + jax.nn.silu(second_sum)).astype(jnp.bfloat16)
    second_wide = second_hidden.astype(jnp.float32)
    third_sum = jnp.zeros(values.shape, jnp.float32)
    for row_tap in range(3):
        for time_tap in range(3):
            third_sum = third_sum + jnp.einsum('i,ixt->xt', conv_out[row_tap, time_tap].astype(jnp.float32), shifted(second_wide, row_tap - 1, time_tap - 1), precision=lax.Precision.HIGHEST)
    return (values + third_sum).astype(jnp.bfloat16)

def reference(predicted, observed, data_weight, bin_ids, offset_slots, conv_in, conv_mid, conv_out):
    panel_cell = (bin_ids * OFFS + offset_slots).astype(jnp.int32)
    panels = jnp.zeros((BINS * OFFS, NT), jnp.bfloat16).at[panel_cell].set(predicted).reshape(BINS, OFFS, NT)
    filtered = lax.map(lambda panel: network(panel, conv_in, conv_mid, conv_out), panels)
    gathered = filtered.reshape(BINS * OFFS, NT)[panel_cell]
    misfit = data_weight * (gathered.astype(jnp.float32) - observed)
    mean_square = jnp.mean(misfit * misfit)
    return (misfit * lax.rsqrt(mean_square + 1e-05)).astype(jnp.bfloat16)
```

```python
import jax
import jax.numpy as jnp
from jax import lax
from jax.experimental import pallas as pl
from jax.experimental.pallas import tpu as pltpu
from jax.sharding import PartitionSpec as P

OFFS = 64
CHAN = 48
SEGS = 8
HALF = (OFFS // 2) * CHAN
WIDE = HALF + 256
TILE = 256


def kernel_body(
    span, chunk_a, chunk_b, p3_ref, w_in_ref, w_mid_ref, w_out_ref, out_ref, h1_ref, z_ref
):
    blk = 2 * SEGS
    n_first = (span + 10) * blk
    n_second = (span + 2) * blk
    tiles = HALF // TILE
    zero_cols = jnp.zeros((n_first, 128), jnp.bfloat16)
    for parity in range(2):
        h1_ref[:, pl.ds(parity * WIDE, 128)] = zero_cols
        h1_ref[:, pl.ds(parity * WIDE + 128 + HALF, 128)] = zero_cols

    @pl.loop(0, n_first // chunk_a)
    def _(step):
        rows = pl.ds(pl.multiple_of(step * chunk_a, 16), chunk_a)
        window = p3_ref[rows, :]
        for parity in range(2):
            for tile in range(tiles):
                half = jnp.dot(
                    window,
                    w_in_ref[:, pl.ds(parity * HALF + tile * TILE, TILE)],
                    preferred_element_type=jnp.float32,
                )
                h1_ref[rows, pl.ds(parity * WIDE + 128 + tile * TILE, TILE)] = (
                    half + half * jnp.tanh(half)
                ).astype(jnp.bfloat16)

    seg = lax.broadcasted_iota(jnp.int32, (blk, 1), 0) % SEGS
    for b in range(5):
        head = pl.ds(b * blk, blk)
        h1_ref[head, :] = jnp.where(seg == 0, 0.0, h1_ref[head, :].astype(jnp.float32)).astype(
            jnp.bfloat16
        )
        tail = pl.ds((span + 5 + b) * blk, blk)
        h1_ref[tail, :] = jnp.where(
            seg == SEGS - 1, 0.0, h1_ref[tail, :].astype(jnp.float32)
        ).astype(jnp.bfloat16)

    @pl.loop(0, n_second // chunk_b)
    def _(step):
        base = pl.multiple_of(step * chunk_b, 16)
        total = jnp.zeros((chunk_b, 3 * OFFS), jnp.float32)
        for parity in range(2):
            for tile in range(tiles):
                half = jnp.zeros((chunk_b, TILE), jnp.float32)
                for tap in range(3):
                    half = half + jnp.dot(
                        h1_ref[
                            pl.ds(base + 4 * blk * tap, chunk_b),
                            pl.ds(parity * WIDE + tile * TILE, 512),
                        ],
                        w_mid_ref[tile % 3, pl.ds(tap * 512, 512), :],
                        preferred_element_type=jnp.float32,
                    )
                first = h1_ref[
                    pl.ds(base + 4 * blk, chunk_b),
                    pl.ds(parity * WIDE + 128 + tile * TILE, TILE),
                ].astype(jnp.float32)
                second = (first + (half + half * jnp.tanh(half))).astype(jnp.bfloat16)
                total = total + jnp.dot(
                    second,
                    w_out_ref[pl.ds(parity * HALF + tile * TILE, TILE), :],
                    preferred_element_type=jnp.float32,
                )
        z_ref[pl.ds(base, chunk_b), :] = total

    z_ref[pl.ds(0, blk), :] = jnp.where(seg == 0, 0.0, z_ref[pl.ds(0, blk), :])
    last = pl.ds((span + 1) * blk, blk)
    z_ref[last, :] = jnp.where(seg == SEGS - 1, 0.0, z_ref[last, :])

    n_out = span * blk

    @pl.loop(0, 8)
    def _(step):
        size = n_out // 8
        base = pl.multiple_of(step * size, 16)
        left = z_ref[pl.ds(base, size), :][:, 0:OFFS]
        mid = z_ref[pl.ds(base + blk, size), :][:, OFFS : 2 * OFFS]
        right = z_ref[pl.ds(base + 2 * blk, size), :][:, 2 * OFFS : 3 * OFFS]
        centre = p3_ref[pl.ds(base + 5 * blk, size), :].astype(jnp.float32)[:, OFFS : 2 * OFFS]
        out_ref[pl.ds(base, size), :] = (centre + (left + mid + right)).astype(jnp.bfloat16)


def largest_chunk(blocks, most):
    return max(d for d in range(1, most + 1) if blocks % d == 0)


def band_weights(conv_in, conv_mid, conv_out):
    half = jnp.bfloat16(0.5)
    offs = jnp.arange(OFFS)
    order = jnp.concatenate([offs[0::2], offs[1::2]])
    taps = jnp.arange(3)
    near = (order[:, None] - offs[None, :])[None]
    pick_in = (-near + 1 == taps[:, None, None]).astype(jnp.bfloat16)
    pick_out = (near + 1 == taps[:, None, None]).astype(jnp.bfloat16)
    w_in = jnp.einsum("alp,adc->dplc", pick_in, conv_in * half).reshape(3 * OFFS, OFFS * CHAN)
    w_out = jnp.einsum("alo,adc->lcdo", pick_out, conv_out).reshape(OFFS * CHAN, 3 * OFFS)
    scaled = conv_mid * half
    tiles = []
    for m in range(3):
        x = jnp.arange(512) + 256 * m - 128
        y = jnp.arange(256) + 256 * m
        rows = (x[:, None] % CHAN == jnp.arange(CHAN)[None]).astype(jnp.bfloat16)
        cols = (jnp.arange(CHAN)[:, None] == y[None] % CHAN).astype(jnp.bfloat16)
        tap = (x // CHAN)[:, None] - (y // CHAN)[None] + 1
        spread = jnp.einsum("xc,adce->adxe", rows, scaled)
        spread = jnp.einsum("adxe,ey->adxy", spread, cols)
        banded = jnp.where(tap[None] == 0, spread[0], jnp.bfloat16(0))
        banded = jnp.where(tap[None] == 1, spread[1], banded)
        banded = jnp.where(tap[None] == 2, spread[2], banded)
        tiles.append(banded.reshape(1536, 256))
    return w_in, jnp.stack(tiles), w_out


def filter_rows(panels, weights):
    bins, offs, samples = panels.shape
    span = samples // SEGS
    blk = bins * SEGS
    padded = jnp.pad(panels, ((0, 0), (0, 0), (6, 6)))
    segs = jnp.stack(
        [padded[:, :, s * span : s * span + span + 12] for s in range(SEGS)], axis=1
    )
    ext = segs.transpose(3, 0, 1, 2).reshape(span + 12, blk, offs)
    p3 = jnp.concatenate([ext[0 : span + 10], ext[1 : span + 11], ext[2 : span + 12]], axis=-1)
    p3 = p3.reshape((span + 10) * blk, 3 * offs)
    chunk_a = largest_chunk(span + 10, 40) * blk
    chunk_b = largest_chunk(span + 2, 44) * blk

    def body(*refs):
        kernel_body(span, chunk_a, chunk_b, *refs)

    return pl.pallas_call(
        body,
        out_shape=jax.ShapeDtypeStruct((span * blk, offs), jnp.bfloat16),
        in_specs=[pl.BlockSpec(memory_space=pltpu.VMEM)] * 4,
        out_specs=pl.BlockSpec(memory_space=pltpu.VMEM),
        scratch_shapes=[
            pltpu.VMEM(((span + 10) * blk, 2 * WIDE), jnp.bfloat16),
            pltpu.VMEM(((span + 2) * blk, 3 * offs), jnp.float32),
        ],
        compiler_params=pltpu.CompilerParams(vmem_limit_bytes=60 * 1024 * 1024),
        name="panel_filter",
    )(p3, *weights)


def local(predicted, observed, data_weight, bin_ids, offset_slots, conv_in, conv_mid, conv_out):
    tr_dev, samples = predicted.shape
    owners = lax.axis_size("bin")
    bin_dev = tr_dev // OFFS
    capacity = max(bin_dev, 2 * tr_dev // owners)
    slots = owners * capacity
    owner_dev = bin_ids // bin_dev
    local_bin = bin_ids % bin_dev
    row_index = jnp.arange(tr_dev, dtype=jnp.int32)
    earlier = row_index[None, :] < row_index[:, None]
    same_owner = owner_dev[:, None] == owner_dev[None, :]
    position = jnp.sum((same_owner & earlier).astype(jnp.int32), axis=1)
    send_slot = owner_dev * capacity + position
    panel_cell = local_bin * OFFS + offset_slots
    send_hit = jnp.arange(slots, dtype=jnp.int32)[:, None] == send_slot[None, :]
    send_pick = send_hit.astype(jnp.bfloat16)
    outgoing = jnp.dot(send_pick, predicted, preferred_element_type=jnp.float32)
    outgoing = outgoing.astype(jnp.bfloat16).reshape(owners, capacity, samples)
    outgoing_cells = (
        jnp.sum(jnp.where(send_hit, panel_cell[None, :] + 1, 0), axis=1) - 1
    ).reshape(owners, capacity)
    arrived_cells = lax.all_to_all(
        outgoing_cells, "bin", split_axis=0, concat_axis=0, tiled=True
    )
    arrived = lax.all_to_all(outgoing, "bin", split_axis=0, concat_axis=0, tiled=True)
    weights = band_weights(conv_in, conv_mid, conv_out)
    cells = jnp.arange(tr_dev, dtype=jnp.int32)
    cell_pick = (arrived_cells.reshape(-1)[:, None] == cells[None, :]).astype(jnp.bfloat16)
    panels = jnp.einsum(
        "sc,st->ct", cell_pick, arrived.reshape(slots, samples), preferred_element_type=jnp.float32
    )
    panels = panels.astype(jnp.bfloat16).reshape(bin_dev, OFFS, samples)
    rows = filter_rows(panels, weights).reshape(samples // SEGS, bin_dev, SEGS, OFFS)
    filtered = rows.transpose(1, 3, 2, 0).reshape(tr_dev, samples)
    answer = jnp.dot(cell_pick, filtered, preferred_element_type=jnp.float32)
    answer = answer.astype(jnp.bfloat16).reshape(owners, capacity, samples)
    returned = lax.all_to_all(answer, "bin", split_axis=0, concat_axis=0, tiled=True)
    own_rows = jnp.einsum(
        "sr,st->rt",
        send_pick,
        returned.reshape(slots, samples),
        preferred_element_type=jnp.float32,
    )
    misfit = data_weight * (own_rows - observed)
    misfit_total = lax.psum(jnp.sum(misfit * misfit), "bin")
    mean_square = misfit_total / (tr_dev * owners * samples)
    return (misfit * lax.rsqrt(mean_square + 1e-05)).astype(jnp.bfloat16)


def solution(mesh):
    in_specs = (
        P(("line", "bin"), None),
        P(("line", "bin"), None),
        P(("line", "bin"), None),
        P(("line", "bin")),
        P(("line", "bin")),
        P(),
        P(),
        P(),
    )
    out_specs = P(("line", "bin"), None)
    return jax.shard_map(local, mesh=mesh, in_specs=in_specs, out_specs=out_specs, check_vma=False)
```

```python
import jax
import jax.numpy as jnp
from jax import lax
from jax.experimental import pallas as pl
from jax.experimental.pallas import tpu as pltpu
from jax.sharding import PartitionSpec as P

OFFS = 64
CHAN = 48
SEGS = 16
MOST = 46
HALF = (OFFS // 2) * CHAN
WIDE = HALF + 256
TILE = 256


def kernel_body(
    span,
    chunk_a,
    chunk_b,
    ext_ref,
    w_in_ref,
    w_mid0_ref,
    w_mid1_ref,
    w_mid2_ref,
    w_out_ref,
    out_ref,
    p3_ref,
    h1_ref,
    z_ref,
):
    w_mid_refs = (w_mid0_ref, w_mid1_ref, w_mid2_ref)
    blk = SEGS
    n_first = (span + 10) * blk
    n_second = (span + 2) * blk
    tiles = HALF // TILE
    zero_cols = jnp.zeros((n_first, 128), jnp.bfloat16)
    for tap in range(3):
        p3_ref[:, pl.ds(tap * OFFS, OFFS)] = ext_ref[pl.ds(tap * blk, n_first), :]
    for parity in range(2):
        h1_ref[:, pl.ds(parity * WIDE, 128)] = zero_cols
        h1_ref[:, pl.ds(parity * WIDE + 128 + HALF, 128)] = zero_cols

    @pl.loop(0, n_first // chunk_a)
    def _(step):
        rows = pl.ds(pl.multiple_of(step * chunk_a, 16), chunk_a)
        window = p3_ref[rows, :]
        for parity in range(2):
            for tile in range(tiles):
                half = jnp.dot(
                    window,
                    w_in_ref[:, pl.ds(parity * HALF + tile * TILE, TILE)],
                    preferred_element_type=jnp.float32,
                )
                h1_ref[rows, pl.ds(parity * WIDE + 128 + tile * TILE, TILE)] = (
                    half + half * jnp.tanh(half)
                ).astype(jnp.bfloat16)

    seg = lax.broadcasted_iota(jnp.int32, (blk, 1), 0)
    for b in range(5):
        head = pl.ds(b * blk, blk)
        h1_ref[head, :] = jnp.where(seg == 0, 0.0, h1_ref[head, :].astype(jnp.float32)).astype(
            jnp.bfloat16
        )
        tail = pl.ds((span + 5 + b) * blk, blk)
        h1_ref[tail, :] = jnp.where(
            seg == SEGS - 1, 0.0, h1_ref[tail, :].astype(jnp.float32)
        ).astype(jnp.bfloat16)

    @pl.loop(0, n_second // chunk_b)
    def _(step):
        base = pl.multiple_of(step * chunk_b, 16)
        total = jnp.zeros((chunk_b, 3 * OFFS), jnp.float32)
        for parity in range(2):
            for tile in range(tiles):
                half = jnp.zeros((chunk_b, TILE), jnp.float32)
                for tap in range(3):
                    half = half + jnp.dot(
                        h1_ref[
                            pl.ds(base + 4 * blk * tap, chunk_b),
                            pl.ds(parity * WIDE + tile * TILE, 512),
                        ],
                        w_mid_refs[tile % 3][pl.ds(tap * 512, 512), :],
                        preferred_element_type=jnp.float32,
                    )
                first = h1_ref[
                    pl.ds(base + 4 * blk, chunk_b),
                    pl.ds(parity * WIDE + 128 + tile * TILE, TILE),
                ].astype(jnp.float32)
                second = (first + (half + half * jnp.tanh(half))).astype(jnp.bfloat16)
                total = total + jnp.dot(
                    second,
                    w_out_ref[pl.ds(parity * HALF + tile * TILE, TILE), :],
                    preferred_element_type=jnp.float32,
                )
        z_ref[pl.ds(base, chunk_b), :] = total

    z_ref[pl.ds(0, blk), :] = jnp.where(seg == 0, 0.0, z_ref[pl.ds(0, blk), :])
    last = pl.ds((span + 1) * blk, blk)
    z_ref[last, :] = jnp.where(seg == SEGS - 1, 0.0, z_ref[last, :])

    n_out = span * blk

    @pl.loop(0, 8)
    def _(step):
        size = n_out // 8
        base = pl.multiple_of(step * size, 16)
        left = z_ref[pl.ds(base, size), :][:, 0:OFFS]
        mid = z_ref[pl.ds(base + blk, size), :][:, OFFS : 2 * OFFS]
        right = z_ref[pl.ds(base + 2 * blk, size), :][:, 2 * OFFS : 3 * OFFS]
        centre = p3_ref[pl.ds(base + 5 * blk, size), :].astype(jnp.float32)[:, OFFS : 2 * OFFS]
        out_ref[pl.ds(base, size), :] = (centre + (left + mid + right)).astype(jnp.bfloat16)


def largest_chunk(blocks, most):
    return max(d for d in range(1, most + 1) if blocks % d == 0)


def band_weights(conv_in, conv_mid, conv_out):
    lane = jnp.arange(OFFS * CHAN)
    place = lane // CHAN
    offset = 2 * (place % (OFFS // 2)) + place // (OFFS // 2)
    spread = (jnp.arange(CHAN)[:, None] == (lane % CHAN)[None]).astype(jnp.bfloat16)
    zero = jnp.bfloat16(0)
    half = jnp.bfloat16(0.5)
    others = jnp.arange(OFFS)

    near = others[:, None] - offset[None, :] + 1
    wide_in = jnp.dot((conv_in * half).reshape(9, CHAN), spread).reshape(3, 3, 1, OFFS * CHAN)
    w_in = zero
    for a in range(3):
        w_in = jnp.where((near == a)[None], wide_in[a], w_in)
    w_in = w_in.reshape(3 * OFFS, OFFS * CHAN)

    near = offset[:, None] - jnp.tile(others, 3)[None, :] + 1
    w_out = zero
    for a in range(3):
        w_out = jnp.where(
            near == a, jnp.dot(spread.T, jnp.repeat(conv_out[a].T, OFFS, axis=1)), w_out
        )

    scaled = conv_mid * half
    tiles = []
    for m in range(3):
        x = jnp.arange(512) + 256 * m - 128
        y = jnp.arange(256) + 256 * m
        rows = (x[:, None] % CHAN == jnp.arange(CHAN)[None]).astype(jnp.bfloat16)
        cols = (jnp.arange(CHAN)[:, None] == y[None] % CHAN).astype(jnp.bfloat16)
        tap = (x // CHAN)[:, None] - (y // CHAN)[None] + 1
        wide = jnp.einsum("adce,ey->adcy", scaled, cols)
        wide = jnp.einsum("xc,adcy->adxy", rows, wide)
        banded = jnp.where(tap[None] == 0, wide[0], zero)
        banded = jnp.where(tap[None] == 1, wide[1], banded)
        banded = jnp.where(tap[None] == 2, wide[2], banded)
        tiles.append(banded.reshape(1536, 256))
    return w_in, tiles[0], tiles[1], tiles[2], w_out


def filter_rows(panel, weights):
    samples, offs = panel.shape
    span = samples // SEGS
    blk = SEGS
    segs = panel.reshape(SEGS, span, offs)
    none = jnp.zeros((1, 6, offs), panel.dtype)
    before = jnp.concatenate([none, segs[:-1, span - 6 :]])
    after = jnp.concatenate([segs[1:, :6], none])
    ext = jnp.concatenate([before, segs, after], axis=1).transpose(1, 0, 2)
    ext = ext.reshape((span + 12) * blk, offs)
    chunk_a = largest_chunk(span + 10, MOST) * blk
    chunk_b = largest_chunk(span + 2, MOST) * blk

    def body(*refs):
        kernel_body(span, chunk_a, chunk_b, *refs)

    rows = pl.pallas_call(
        body,
        out_shape=jax.ShapeDtypeStruct((span * blk, offs), jnp.bfloat16),
        in_specs=[pl.BlockSpec(memory_space=pltpu.VMEM)] * 6,
        out_specs=pl.BlockSpec(memory_space=pltpu.VMEM),
        scratch_shapes=[
            pltpu.VMEM(((span + 10) * blk, 3 * offs), jnp.bfloat16),
            pltpu.VMEM(((span + 10) * blk, 2 * WIDE), jnp.bfloat16),
            pltpu.VMEM(((span + 2) * blk, 3 * offs), jnp.float32),
        ],
        compiler_params=pltpu.CompilerParams(vmem_limit_bytes=48 * 1024 * 1024),
        name="panel_filter",
    )(ext, *weights)
    return rows.reshape(span, SEGS, offs).transpose(1, 0, 2).reshape(samples, offs)


def local(predicted, observed, data_weight, bin_ids, offset_slots, conv_in, conv_mid, conv_out):
    tr_dev, samples = predicted.shape
    owners = lax.axis_size("bin")
    bin_dev = tr_dev // OFFS
    capacity = max(1, tr_dev // owners)
    slots = owners * capacity
    row_index = jnp.arange(tr_dev, dtype=jnp.int32)
    earlier = row_index[None, :] < row_index[:, None]
    same_bin = bin_ids[:, None] == bin_ids[None, :]
    position = jnp.sum((same_bin & earlier).astype(jnp.int32), axis=1)
    owner_slot = (bin_ids // bin_dev) * capacity + position
    local_bin = bin_ids % bin_dev
    mark = jnp.broadcast_to((offset_slots + 1).astype(jnp.bfloat16)[:, None], (tr_dev, 128))
    labelled = jnp.concatenate([predicted, mark], axis=1)
    slot_index = jnp.arange(slots, dtype=jnp.int32)
    offsets = jnp.arange(OFFS, dtype=jnp.int32)

    picks = []
    arrivals = []
    for b in range(bin_dev):
        send_slot = jnp.where(local_bin == b, owner_slot, -1)
        pick = (slot_index[:, None] == send_slot[None, :]).astype(jnp.bfloat16)
        outgoing = jnp.dot(pick, labelled, preferred_element_type=jnp.float32)
        outgoing = outgoing.astype(jnp.bfloat16).reshape(owners, capacity, samples + 128)
        arrived = lax.all_to_all(outgoing, "bin", split_axis=0, concat_axis=0, tiled=True)
        picks.append(pick)
        arrivals.append(arrived.reshape(slots, samples + 128))

    weights = band_weights(conv_in, conv_mid, conv_out)
    own_rows = 0.0
    for b in range(bin_dev):
        cell = arrivals[b][:, samples].astype(jnp.int32) - 1
        cell_pick = (cell[:, None] == offsets[None, :]).astype(jnp.bfloat16)
        panel = jnp.einsum(
            "sc,st->tc",
            cell_pick,
            arrivals[b][:, :samples],
            preferred_element_type=jnp.float32,
        ).astype(jnp.bfloat16)
        filtered = filter_rows(panel, weights)
        answer = jnp.einsum("sc,tc->st", cell_pick, filtered, preferred_element_type=jnp.float32)
        answer = answer.astype(jnp.bfloat16).reshape(owners, capacity, samples)
        returned = lax.all_to_all(answer, "bin", split_axis=0, concat_axis=0, tiled=True)
        own_rows = own_rows + jnp.einsum(
            "sr,st->rt",
            picks[b],
            returned.reshape(slots, samples),
            preferred_element_type=jnp.float32,
        )
    misfit = data_weight * (own_rows - observed)
    share = jnp.broadcast_to(jnp.sum(misfit * misfit), (owners, 1, 128))
    shares = lax.all_to_all(share, "bin", split_axis=0, concat_axis=0, tiled=True)
    misfit_total = jnp.sum(shares[:, 0, 0])
    mean_square = misfit_total / (tr_dev * owners * samples)
    return (misfit * lax.rsqrt(mean_square + 1e-05)).astype(jnp.bfloat16)


def solution(mesh):
    in_specs = (
        P(("line", "bin"), None),
        P(("line", "bin"), None),
        P(("line", "bin"), None),
        P(("line", "bin")),
        P(("line", "bin")),
        P(),
        P(),
        P(),
    )
    out_specs = P(("line", "bin"), None)
    return jax.shard_map(local, mesh=mesh, in_specs=in_specs, out_specs=out_specs, check_vma=False)
```

```python
import jax
import jax.numpy as jnp
from jax import lax
from jax.experimental import pallas as pl
from jax.experimental.pallas import tpu as pltpu
from jax.sharding import PartitionSpec as P

OFFS = 64
CHAN = 48
SEGS = 16
MOST = 46
HALF = (OFFS // 2) * CHAN
WIDE = HALF + 256
TILE = 256


def kernel_body(
    span,
    chunk_a,
    chunk_b,
    ext_ref,
    w_in_ref,
    w_mid0_ref,
    w_mid1_ref,
    w_mid2_ref,
    w_out_ref,
    out_ref,
    p3_ref,
    h1_ref,
    z_ref,
):
    w_mid_refs = (w_mid0_ref, w_mid1_ref, w_mid2_ref)
    blk = SEGS
    n_first = (span + 10) * blk
    n_second = (span + 2) * blk
    tiles = HALF // TILE
    zero_cols = jnp.zeros((n_first, 128), jnp.bfloat16)
    for tap in range(3):
        p3_ref[:, pl.ds(tap * OFFS, OFFS)] = ext_ref[pl.ds(tap * blk, n_first), :]
    for parity in range(2):
        h1_ref[:, pl.ds(parity * WIDE, 128)] = zero_cols
        h1_ref[:, pl.ds(parity * WIDE + 128 + HALF, 128)] = zero_cols

    @pl.loop(0, n_first // chunk_a)
    def _(step):
        rows = pl.ds(pl.multiple_of(step * chunk_a, 16), chunk_a)
        window = p3_ref[rows, :]
        for parity in range(2):
            for tile in range(tiles):
                half = jnp.dot(
                    window,
                    w_in_ref[:, pl.ds(parity * HALF + tile * TILE, TILE)],
                    preferred_element_type=jnp.float32,
                )
                h1_ref[rows, pl.ds(parity * WIDE + 128 + tile * TILE, TILE)] = (
                    half + half * jnp.tanh(half)
                ).astype(jnp.bfloat16)

    seg = lax.broadcasted_iota(jnp.int32, (blk, 1), 0)
    for b in range(5):
        head = pl.ds(b * blk, blk)
        h1_ref[head, :] = jnp.where(seg == 0, 0.0, h1_ref[head, :].astype(jnp.float32)).astype(
            jnp.bfloat16
        )
        tail = pl.ds((span + 5 + b) * blk, blk)
        h1_ref[tail, :] = jnp.where(
            seg == SEGS - 1, 0.0, h1_ref[tail, :].astype(jnp.float32)
        ).astype(jnp.bfloat16)

    @pl.loop(0, n_second // chunk_b)
    def _(step):
        base = pl.multiple_of(step * chunk_b, 16)
        total = jnp.zeros((chunk_b, 3 * OFFS), jnp.float32)
        for parity in range(2):
            for tile in range(tiles):
                half = jnp.zeros((chunk_b, TILE), jnp.float32)
                for tap in range(3):
                    half = half + jnp.dot(
                        h1_ref[
                            pl.ds(base + 4 * blk * tap, chunk_b),
                            pl.ds(parity * WIDE + tile * TILE, 512),
                        ],
                        w_mid_refs[tile % 3][pl.ds(tap * 512, 512), :],
                        preferred_element_type=jnp.float32,
                    )
                first = h1_ref[
                    pl.ds(base + 4 * blk, chunk_b),
                    pl.ds(parity * WIDE + 128 + tile * TILE, TILE),
                ].astype(jnp.float32)
                second = (first + (half + half * jnp.tanh(half))).astype(jnp.bfloat16)
                total = total + jnp.dot(
                    second,
                    w_out_ref[pl.ds(parity * HALF + tile * TILE, TILE), :],
                    preferred_element_type=jnp.float32,
                )
        z_ref[pl.ds(base, chunk_b), :] = total

    z_ref[pl.ds(0, blk), :] = jnp.where(seg == 0, 0.0, z_ref[pl.ds(0, blk), :])
    last = pl.ds((span + 1) * blk, blk)
    z_ref[last, :] = jnp.where(seg == SEGS - 1, 0.0, z_ref[last, :])

    n_out = span * blk

    @pl.loop(0, 8)
    def _(step):
        size = n_out // 8
        base = pl.multiple_of(step * size, 16)
        left = z_ref[pl.ds(base, size), :][:, 0:OFFS]
        mid = z_ref[pl.ds(base + blk, size), :][:, OFFS : 2 * OFFS]
        right = z_ref[pl.ds(base + 2 * blk, size), :][:, 2 * OFFS : 3 * OFFS]
        centre = p3_ref[pl.ds(base + 5 * blk, size), :].astype(jnp.float32)[:, OFFS : 2 * OFFS]
        out_ref[pl.ds(base, size), :] = (centre + (left + mid + right)).astype(jnp.bfloat16)


def largest_chunk(blocks, most):
    return max(d for d in range(1, most + 1) if blocks % d == 0)


def by_chan(v):
    return (v * 43691) >> 21


def one_hot(remainder, index, value):
    return jnp.where(remainder == index, value, 0.0).astype(jnp.bfloat16)


def weights_body(
    conv_in_ref,
    conv_mid_ref,
    conv_out_ref,
    w_in_ref,
    w_mid0_ref,
    w_mid1_ref,
    w_mid2_ref,
    w_out_ref,
):
    f32 = jnp.float32

    def iota(shape, axis):
        return lax.broadcasted_iota(jnp.int32, shape, axis)

    def offset_of(place):
        return jnp.where(place < OFFS // 2, 2 * place, 2 * place - OFFS + 1)

    others = iota((OFFS, 1), 0) + 1

    @pl.loop(0, 6)
    def _(part):
        base = pl.multiple_of(part * 512, 512)
        lane = iota((1, 512), 1) + base
        place = by_chan(lane)
        near = others - offset_of(place)
        spread = one_hot(lane - CHAN * place, iota((CHAN, 1), 0), 0.5)
        wide = [jnp.dot(conv_in_ref[a], spread, preferred_element_type=f32) for a in range(3)]
        for d in range(3):
            value = jnp.zeros((OFFS, 512), f32)
            for a in range(3):
                value = jnp.where(near == a, wide[a][d : d + 1, :], value)
            w_in_ref[pl.ds(d * OFFS, OFFS), pl.ds(base, 512)] = value.astype(jnp.bfloat16)

    for m, w_mid_ref in enumerate((w_mid0_ref, w_mid1_ref, w_mid2_ref)):
        x = iota((512, 1), 0) + (256 * m - 128 + 3 * CHAN)
        y = iota((1, TILE), 1) + 256 * m
        cell_x = by_chan(x)
        cell_y = by_chan(y)
        rows = one_hot(x - CHAN * cell_x, iota((1, CHAN), 1), 1.0)
        cols = one_hot(y - CHAN * cell_y, iota((CHAN, 1), 0), 0.5)
        wide = jnp.dot(conv_mid_ref[...], cols, preferred_element_type=f32)
        wide = wide.astype(jnp.bfloat16)
        tap = cell_x - 2 - cell_y
        for d in range(3):
            value = jnp.zeros((512, TILE), f32)
            for a in range(3):
                start = (a * 3 + d) * CHAN
                part = jnp.dot(
                    rows, wide[start : start + CHAN, :], preferred_element_type=f32
                )
                value = jnp.where(tap == a, part, value)
            w_mid_ref[pl.ds(d * 512, 512), :] = value.astype(jnp.bfloat16)

    triple = iota((1, 3 * OFFS), 1)
    group = triple // OFFS
    wide_out = []
    for a in range(3):
        value = jnp.zeros((CHAN, 3 * OFFS), f32)
        for d in range(3):
            value = jnp.where(group == d, conv_out_ref[a, :, d : d + 1].astype(f32), value)
        wide_out.append(value.astype(jnp.bfloat16))

    @pl.loop(0, 6)
    def _(part):
        base = pl.multiple_of(part * 512, 512)
        lane = iota((512, 1), 0) + base
        place = by_chan(lane)
        near = offset_of(place) + 1 - (triple - OFFS * group)
        across = one_hot(lane - CHAN * place, iota((1, CHAN), 1), 1.0)
        value = jnp.zeros((512, 3 * OFFS), f32)
        for a in range(3):
            value = jnp.where(
                near == a, jnp.dot(across, wide_out[a], preferred_element_type=f32), value
            )
        w_out_ref[pl.ds(base, 512), :] = value.astype(jnp.bfloat16)


def band_weights(conv_in, conv_mid, conv_out):
    bf16 = jnp.bfloat16
    mid = jax.ShapeDtypeStruct((1536, TILE), bf16)
    return pl.pallas_call(
        weights_body,
        out_shape=(
            jax.ShapeDtypeStruct((3 * OFFS, OFFS * CHAN), bf16),
            mid,
            mid,
            mid,
            jax.ShapeDtypeStruct((OFFS * CHAN, 3 * OFFS), bf16),
        ),
        in_specs=[pl.BlockSpec(memory_space=pltpu.VMEM)] * 3,
        out_specs=[pl.BlockSpec(memory_space=pltpu.VMEM)] * 5,
        compiler_params=pltpu.CompilerParams(vmem_limit_bytes=40 * 1024 * 1024),
        name="band_weights",
    )(conv_in, conv_mid.reshape(9 * CHAN, CHAN), conv_out.transpose(0, 2, 1))


def filter_rows(panel, weights):
    samples, offs = panel.shape
    span = samples // SEGS
    blk = SEGS
    segs = panel.reshape(SEGS, span, offs)
    none = jnp.zeros((1, 6, offs), panel.dtype)
    before = jnp.concatenate([none, segs[:-1, span - 6 :]])
    after = jnp.concatenate([segs[1:, :6], none])
    ext = jnp.concatenate([before, segs, after], axis=1).transpose(1, 0, 2)
    ext = ext.reshape((span + 12) * blk, offs)
    chunk_a = largest_chunk(span + 10, MOST) * blk
    chunk_b = largest_chunk(span + 2, MOST) * blk

    def body(*refs):
        kernel_body(span, chunk_a, chunk_b, *refs)

    rows = pl.pallas_call(
        body,
        out_shape=jax.ShapeDtypeStruct((span * blk, offs), jnp.bfloat16),
        in_specs=[pl.BlockSpec(memory_space=pltpu.VMEM)] * 6,
        out_specs=pl.BlockSpec(memory_space=pltpu.VMEM),
        scratch_shapes=[
            pltpu.VMEM(((span + 10) * blk, 3 * offs), jnp.bfloat16),
            pltpu.VMEM(((span + 10) * blk, 2 * WIDE), jnp.bfloat16),
            pltpu.VMEM(((span + 2) * blk, 3 * offs), jnp.float32),
        ],
        compiler_params=pltpu.CompilerParams(vmem_limit_bytes=48 * 1024 * 1024),
        name="panel_filter",
    )(ext, *weights)
    return rows.reshape(span, SEGS, offs).transpose(1, 0, 2).reshape(samples, offs)


def local(predicted, observed, data_weight, bin_ids, offset_slots, conv_in, conv_mid, conv_out):
    tr_dev, samples = predicted.shape
    owners = lax.axis_size("bin")
    bin_dev = tr_dev // OFFS
    capacity = max(1, tr_dev // owners)
    slots = owners * capacity
    row_index = jnp.arange(tr_dev, dtype=jnp.int32)
    earlier = row_index[None, :] < row_index[:, None]
    same_bin = bin_ids[:, None] == bin_ids[None, :]
    position = jnp.sum((same_bin & earlier).astype(jnp.int32), axis=1)
    owner_slot = (bin_ids // bin_dev) * capacity + position
    local_bin = bin_ids % bin_dev
    mark = jnp.broadcast_to((offset_slots + 1).astype(jnp.bfloat16)[:, None], (tr_dev, 128))
    labelled = jnp.concatenate([predicted, mark], axis=1)
    slot_index = jnp.arange(slots, dtype=jnp.int32)
    offsets = jnp.arange(OFFS, dtype=jnp.int32)

    picks = []
    arrivals = []
    for b in range(bin_dev):
        send_slot = jnp.where(local_bin == b, owner_slot, -1)
        pick = (slot_index[:, None] == send_slot[None, :]).astype(jnp.bfloat16)
        outgoing = jnp.dot(pick, labelled, preferred_element_type=jnp.float32)
        outgoing = outgoing.astype(jnp.bfloat16).reshape(owners, capacity, samples + 128)
        if b == 0:
            outgoing, conv_in, conv_mid, conv_out = lax.optimization_barrier(
                (outgoing, conv_in, conv_mid, conv_out)
            )
            weights = band_weights(conv_in, conv_mid, conv_out)
        else:
            outgoing, weights = lax.optimization_barrier((outgoing, weights))
        arrived = lax.all_to_all(outgoing, "bin", split_axis=0, concat_axis=0, tiled=True)
        picks.append(pick)
        arrivals.append(arrived.reshape(slots, samples + 128))

    own_rows = 0.0
    for b in range(bin_dev):
        cell = arrivals[b][:, samples].astype(jnp.int32) - 1
        cell_pick = (cell[:, None] == offsets[None, :]).astype(jnp.bfloat16)
        panel = jnp.einsum(
            "sc,st->tc",
            cell_pick,
            arrivals[b][:, :samples],
            preferred_element_type=jnp.float32,
        ).astype(jnp.bfloat16)
        filtered = filter_rows(panel, weights)
        answer = jnp.einsum("sc,tc->st", cell_pick, filtered, preferred_element_type=jnp.float32)
        answer = answer.astype(jnp.bfloat16).reshape(owners, capacity, samples)
        returned = lax.all_to_all(answer, "bin", split_axis=0, concat_axis=0, tiled=True)
        own_rows = own_rows + jnp.einsum(
            "sr,st->rt",
            picks[b],
            returned.reshape(slots, samples),
            preferred_element_type=jnp.float32,
        )
    misfit = data_weight * (own_rows - observed)
    share = jnp.broadcast_to(jnp.sum(misfit * misfit), (owners, 1, 128))
    shares = lax.all_to_all(share, "bin", split_axis=0, concat_axis=0, tiled=True)
    misfit_total = jnp.sum(shares[:, 0, 0])
    mean_square = misfit_total / (tr_dev * owners * samples)
    return (misfit * lax.rsqrt(mean_square + 1e-05)).astype(jnp.bfloat16)


def solution(mesh):
    in_specs = (
        P(("line", "bin"), None),
        P(("line", "bin"), None),
        P(("line", "bin"), None),
        P(("line", "bin")),
        P(("line", "bin")),
        P(),
        P(),
        P(),
    )
    out_specs = P(("line", "bin"), None)
    return jax.shard_map(local, mesh=mesh, in_specs=in_specs, out_specs=out_specs, check_vma=False)
```
